32 devices in a mesh: tm: 8 (over z, x), space: 4 (over y, core).
Axes of the slice: x: 2, y: 2, z: 4, core: 2. Of those that a mesh axis runs over, the one named last changes fastest.
Arguments:
- tokens: bfloat16 [16384, 2240], P(('tm', 'space')), may hold values from -8 to 8, as said below
- tangents: bfloat16 [16384, 2240], P(('tm', 'space')), may hold values from -6 to 6
- w_query: bfloat16 [2240, 560], replicated, may hold values from -0.125 to 0.125
- w_key: bfloat16 [2240, 560], replicated, may hold values from -0.125 to 0.125
- w_value: bfloat16 [2240, 560], replicated, may hold values from -0.125 to 0.125
Outputs:
- attended: bfloat16 [16384, 560], P(('tm', 'space'))
- attended_tangent: bfloat16 [16384, 560], P(('tm', 'space'))
The draws below stay inside these ranges and needn't reach their ends.
Inputs may be any that keep to these rules, and one draw needn't show every extreme that they name: `tokens`: activations of every token, each spread about an offset that varies by feature and by group of rows.
All inputs are finite; a program needn't handle non-finite values.
Results may differ from the reference program's by a relative error of at most 0.018.
Values sent between devices are 32-bit elements; how exact they have to be, the bound alone decides.
A program may use at most 64 MiB of HBM per device.

```python
import jax
import jax.numpy as jnp
from jax import lax

D = 2240
HD = 112
HEADS = 5
TOK_DEV = 512
BLOCK_TOK = 2048
TOKENS = 16384


def draw_tokens(key, part):
    first, second = jax.random.split(jax.random.fold_in(key, 11), 2)
    group_rows = max(TOK_DEV // 2, 1)
    groups = (TOKENS + group_rows - 1) // group_rows
    offsets = jax.random.uniform(second, (groups, D), jnp.float32, -1.5, 1.5)
    base = jnp.clip(jax.random.normal(first, (TOKENS, D), jnp.float32), -4.0, 4.0)
    group_index = (jnp.arange(TOKENS) // group_rows).astype(jnp.int32)
    return jnp.clip(base + offsets[group_index], -8.0, 8.0).astype(jnp.bfloat16)


def level_of(rng, extent, cuts, smallest, largest):
    def one(position, shards_of):
        heights = jax.random.uniform(jax.random.fold_in(jax.random.fold_in(rng, 6), position), (shards_of,), jnp.float32, smallest / len(cuts), largest / len(cuts))
        return jnp.repeat(jnp.exp(heights), extent[position] // shards_of).reshape((-1,) + (1,) * (len(extent) - position - 1))

    level = one(*cuts[0])
    for cut in cuts[1:]:
        level = level * one(*cut)
    return level


def bell_draw(rng, extent, deviation, most, cuts=(), kind=jnp.bfloat16):
    gain = level_of(rng, extent, cuts, -0.22, 0.18) if cuts else 1.0
    values = jax.random.normal(rng, extent, jnp.float32) * deviation * gain
    return jnp.minimum(jnp.maximum(values, -most), most).astype(kind)


def setup_inputs(seed: int = 0) -> dict:
    streams_of = jax.random.split(jax.random.key(seed), 6)
    return {
        "tokens": draw_tokens(jax.random.fold_in(streams_of[5], 71), 0),
        "tangents": bell_draw(streams_of[1], (TOKENS, D), 1.0, 6.0, ((0, 32),)),
        "w_query": bell_draw(streams_of[2], (D, HEADS * HD), D ** -0.5, 0.125),
        "w_key": bell_draw(streams_of[3], (D, HEADS * HD), D ** -0.5, 0.125),
        "w_value": bell_draw(streams_of[4], (D, HEADS * HD), D ** -0.5, 0.125),
    }


epsilon = 1e-6


def project(source, w_query, w_key, w_value):
    return tuple(jnp.dot(source, weight, preferred_element_type=jnp.float32).astype(jnp.bfloat16).reshape(TOKENS // BLOCK_TOK, BLOCK_TOK, HEADS, HD) for weight in (w_query, w_key, w_value))


def reference(tokens, tangents, w_query, w_key, w_value):
    highest = lax.Precision.HIGHEST
    queries, keys, values = project(tokens, w_query, w_key, w_value)
    query_tangent, key_tangent, value_tangent = project(tangents, w_query, w_key, w_value)
    key_feature = jnp.maximum(keys, jnp.zeros_like(keys)).astype(jnp.float32)
    feature_tangent = jnp.where(keys > 0, key_tangent, jnp.zeros_like(key_tangent)).astype(jnp.float32)
    values_wide = values.astype(jnp.float32)
    value_slope = value_tangent.astype(jnp.float32)
    state = jnp.einsum("blhd,blhe->bhde", key_feature, values_wide, precision=highest)
    state_tangent = jnp.einsum("blhd,blhe->bhde", feature_tangent, values_wide, precision=highest) + jnp.einsum("blhd,blhe->bhde", key_feature, value_slope, precision=highest)
    norm_main = jnp.sum(key_feature, axis=1)
    norm_tangent = jnp.sum(feature_tangent, axis=1)
    seen = jnp.cumsum(state, axis=0)
    seen_tangent = jnp.cumsum(state_tangent, axis=0)
    seen_norm = jnp.cumsum(norm_main, axis=0)
    seen_norm_tangent = jnp.cumsum(norm_tangent, axis=0)
    query_feature = jnp.maximum(queries, jnp.zeros_like(queries)).astype(jnp.float32)
    query_slope = jnp.where(queries > 0, query_tangent, jnp.zeros_like(query_tangent)).astype(jnp.float32)
    numer = jnp.einsum("blhd,bhde->blhe", query_feature, seen, precision=highest)
    denom = jnp.einsum("blhd,bhd->blh", query_feature, seen_norm, precision=highest) + epsilon
    numer_tangent = jnp.einsum("blhd,bhde->blhe", query_slope, seen, precision=highest) + jnp.einsum("blhd,bhde->blhe", query_feature, seen_tangent, precision=highest)
    denom_tangent = jnp.einsum("blhd,bhd->blh", query_slope, seen_norm, precision=highest) + jnp.einsum("blhd,bhd->blh", query_feature, seen_norm_tangent, precision=highest)
    denom = denom[..., None]
    denom_tangent = denom_tangent[..., None]
    attended = (numer / denom).astype(jnp.bfloat16).reshape(TOKENS, HEADS * HD)
    attended_tangent = (numer_tangent / denom - numer * denom_tangent / (denom * denom)).astype(jnp.bfloat16).reshape(TOKENS, HEADS * HD)
    return attended, attended_tangent
```

```python
import functools

import jax
import jax.numpy as jnp
from jax import lax
from jax.experimental import pallas as pl
from jax.experimental.pallas import tpu as pltpu
from jax.sharding import PartitionSpec as P

HD = 112
HEADS = 5
WIDE = 128
EPSILON = 1e-06
MESH = pl.DeviceIdType.MESH


def dot(a, b, dims=((1,), (0,))):
    return lax.dot_general(a, b, (dims, ((), ())), preferred_element_type=jnp.float32)


def kernel(
    n_tm, n_space, rows,
    tok_hbm, tan_hbm, wq_hbm, wk_hbm, wv_hbm,
    att_ref, att_t_ref,
    tok, tan, wq, wk, wv, load_sem,
    kbuf, vbuf, ktbuf, vtbuf, qbuf, qtbuf,
    state, r1, abuf, r2, bbuf, r3, erecv, esend, xsend, full,
    s1, q1, s2, q2, s3, q3, s4, q4, s5, q5, s6, q6, s7, q7,
):
    ny, nz = n_space // 2, n_tm // 2
    half, quarter, eighth = rows // 2, rows // n_space, rows // (2 * n_space)
    tm, space = lax.axis_index("tm"), lax.axis_index("space")
    core, y = lax.rem(space, 2), space // 2
    x, z = lax.rem(tm, 2), tm // 2
    core_mate = space + 1 - 2 * core
    x_mate = tm + 1 - 2 * x
    z_next, z_prev = lax.rem(tm + 2, n_tm), lax.rem(tm + n_tm - 2, n_tm)

    def y_mate(k):
        return 2 * lax.rem(y + k, ny) + core

    def load(i, src, dst):
        return pltpu.make_async_copy(src, dst, load_sem.at[i])

    loads = [
        load(0, tok_hbm, tok), load(1, wk_hbm, wk), load(2, wv_hbm, wv),
        load(3, tan_hbm, tan), load(4, wq_hbm, wq),
    ]
    for one in loads:
        one.start()

    barrier = pltpu.get_barrier_semaphore()
    partners = [{"space": core_mate}, {"tm": x_mate}, {"tm": z_next}, {"tm": z_prev}]
    partners += [{"space": y_mate(k)} for k in range(1, ny)]
    for partner in partners:
        pl.semaphore_signal(barrier, inc=1, device_id=partner, device_id_type=MESH)

    def rows_at(start, count):
        return pl.ds(pl.multiple_of(start, 8), count)

    half_mine = core * half
    quarter_mine = half_mine + y * quarter

    def send(src, dst, ssem, rsem, device):
        return pltpu.make_async_remote_copy(
            src_ref=src, dst_ref=dst, send_sem=ssem, recv_sem=rsem,
            device_id=device, device_id_type=MESH,
        )

    def copy1(g):
        return send(
            state.at[g, rows_at((1 - core) * half, half)], r1.at[g],
            s1.at[g], q1.at[g], {"space": core_mate},
        )

    def copy2(g, k):
        return send(
            abuf.at[g, rows_at(lax.rem(y + k, ny) * quarter, quarter)], r2.at[g, k - 1],
            s2.at[g, k - 1], q2.at[g, k - 1], {"space": y_mate(k)},
        )

    def copy3(g):
        return send(
            bbuf.at[g, rows_at((1 - x) * eighth, eighth)], r3.at[g],
            s3.at[g], q3.at[g], {"tm": x_mate},
        )

    def copy4(g):
        return send(esend.at[g], erecv.at[g], s4.at[g], q4.at[g], {"tm": z_next})

    def copy5(g):
        return send(
            xsend.at[g], full.at[g, rows_at(quarter_mine + x * eighth, eighth)],
            s5.at[g], q5.at[g], {"tm": x_mate},
        )

    def copy6(g, k):
        part = full.at[g, rows_at(quarter_mine, quarter)]
        return send(part, part, s6.at[g, k - 1], q6.at[g, k - 1], {"space": y_mate(k)})

    def copy7(g, k):
        part = full.at[g, rows_at(half_mine + lax.rem(y + ny - k, ny) * quarter, quarter)]
        return send(part, part, s7.at[g, k], q7.at[g, k], {"space": core_mate})

    def stage1(g):
        copy1(g).start()

    def stage2(g):
        copy1(g).wait_recv()
        abuf[g] = state[g, rows_at(half_mine, half)] + r1[g]
        for k in range(1, ny):
            copy2(g, k).start()

    def stage3(g):
        total = abuf[g, rows_at(y * quarter, quarter)]
        for k in range(1, ny):
            copy2(g, k).wait_recv()
            total = total + r2[g, k - 1]
        bbuf[g] = total
        copy3(g).start()

    def stage4(g):
        copy3(g).wait_recv()
        own = bbuf[g, rows_at(x * eighth, eighth)]

        @pl.when(z == 0)
        def _():
            erecv[g] = jnp.zeros((eighth, WIDE), jnp.float32)

        @pl.when(z > 0)
        def _():
            copy4(g).wait_recv()

        before, other = erecv[g], r3[g]
        first = before + other
        pair = first + own

        @pl.when(z < nz - 1)
        def _():
            esend[g] = pair
            copy4(g).start()

        mine_first = x == 0
        xsend[g] = jnp.where(mine_first, pair, first)
        copy5(g).start()
        full[g, rows_at(quarter_mine + x * eighth, eighth)] = jnp.where(
            mine_first, before + own, pair
        )

    def stage6(g):
        copy5(g).wait_recv()
        for k in range(1, ny):
            copy6(g, k).start()
        copy7(g, 0).start()

    def stage7(g):
        for k in range(1, ny):
            copy6(g, k).wait_recv()
            copy7(g, k).start()

    def finish(g):
        for k in range(ny):
            copy7(g, k).wait_recv()

    def drain(g):
        copy1(g).wait_send()
        for k in range(1, ny):
            copy2(g, k).wait_send()
            copy6(g, k).wait_send()
        copy3(g).wait_send()

        @pl.when(z < nz - 1)
        def _():
            copy4(g).wait_send()

        copy5(g).wait_send()
        for k in range(ny):
            copy7(g, k).wait_send()

    def project(source, weight, out):
        out[...] = dot(source[...], weight[...]).astype(jnp.bfloat16)

    count = tok.shape[0]

    def head(ref, h):
        return ref[:, h * HD : (h + 1) * HD]

    def values_of(ref, h, fill):
        tail = jnp.where(
            lax.broadcasted_iota(jnp.int32, (count, WIDE - HD), 1) == 0, fill, 0.0
        ).astype(jnp.bfloat16)
        return jnp.concatenate([head(ref, h), tail], axis=1)

    for g in range(2):
        state[g, rows_at(HEADS * HD, rows - HEADS * HD)] = jnp.zeros(
            (rows - HEADS * HD, WIDE), jnp.float32
        )
    loads[0].wait()
    loads[1].wait()
    project(tok, wk, kbuf)
    loads[2].wait()
    project(tok, wv, vbuf)
    over = ((0,), (0,))
    zero = jnp.zeros((), jnp.bfloat16)
    for h in range(HEADS):
        feature = jnp.maximum(head(kbuf, h), zero)
        state[0, h * HD : (h + 1) * HD] = dot(feature, values_of(vbuf, h, 1.0), over)
    pl.semaphore_wait(barrier, len(partners))
    stage1(0)
    loads[3].wait()
    project(tan, wk, ktbuf)
    stage2(0)
    project(tan, wv, vtbuf)
    for h in range(HEADS):
        keys = head(kbuf, h)
        feature = jnp.maximum(keys, zero)
        slope = jnp.where(keys > 0, head(ktbuf, h), zero)
        state[1, h * HD : (h + 1) * HD] = dot(slope, values_of(vbuf, h, 1.0), over) + dot(
            feature, values_of(vtbuf, h, 0.0), over
        )
    stage1(1)
    stage3(0)
    loads[4].wait()
    project(tok, wq, qbuf)
    stage2(1)
    stage4(0)
    project(tan, wq, qtbuf)
    stage3(1)
    stage4(1)
    stage6(0)
    stage7(0)
    stage6(1)
    finish(0)
    stage7(1)
    finish(1)

    pad_rows = jnp.zeros((WIDE - HD, WIDE), jnp.float32)
    pad_lanes = jnp.zeros((count, WIDE - HD), jnp.bfloat16)
    empty = jnp.zeros((WIDE, WIDE), jnp.float32)
    for h in range(HEADS):
        queries = head(qbuf, h)
        feature = jnp.maximum(queries, zero)
        slope = jnp.where(queries > 0, head(qtbuf, h), zero)
        left = jnp.concatenate([feature, pad_lanes, slope, pad_lanes], axis=1)
        seen = jnp.concatenate([full[0, h * HD : (h + 1) * HD], pad_rows], axis=0)
        seen_t = jnp.concatenate([full[1, h * HD : (h + 1) * HD], pad_rows], axis=0)
        right = jnp.concatenate(
            [
                jnp.concatenate([seen, seen_t], axis=1),
                jnp.concatenate([empty, seen], axis=1),
            ],
            axis=0,
        )
        high = right.astype(jnp.bfloat16)
        low = (right - high.astype(jnp.float32)).astype(jnp.bfloat16)
        both = dot(left, high) + dot(left, low)
        main, slant = both[:, :WIDE], both[:, WIDE:]
        inverse = 1.0 / (main[:, HD : HD + 1] + EPSILON)
        denom_t = slant[:, HD : HD + 1]
        attended = main * inverse
        tangent = (slant - attended * denom_t) * inverse
        att_ref[:, h * HD : (h + 1) * HD] = attended[:, :HD].astype(att_ref.dtype)
        att_t_ref[:, h * HD : (h + 1) * HD] = tangent[:, :HD].astype(att_t_ref.dtype)
    for g in range(2):
        drain(g)


def solution(mesh):
    n_tm, n_space = mesh.shape["tm"], mesh.shape["space"]
    ny = n_space // 2
    unit = 8 * 2 * n_space
    rows = (HEADS * HD + unit) // unit * unit

    def step(tokens, tangents, w_query, w_key, w_value):
        count, width = tokens.shape
        out = w_query.shape[1]
        bf16, f32 = jnp.bfloat16, jnp.float32
        quarter, eighth = rows // n_space, rows // (2 * n_space)
        dma = pltpu.SemaphoreType.DMA
        sems = []
        for shape in ((2,), (2, ny - 1), (2,), (2,), (2,), (2, ny - 1), (2, ny)):
            sems += [dma(shape), dma(shape)]
        return tuple(pl.pallas_call(
            functools.partial(kernel, n_tm, n_space, rows),
            out_shape=[jax.ShapeDtypeStruct((count, out), bf16)] * 2,
            in_specs=[pl.BlockSpec(memory_space=pl.ANY)] * 5,
            out_specs=[pl.BlockSpec(memory_space=pltpu.VMEM)] * 2,
            scratch_shapes=[
                pltpu.VMEM((count, width), bf16),
                pltpu.VMEM((count, width), bf16),
                pltpu.VMEM((width, out), bf16),
                pltpu.VMEM((width, out), bf16),
                pltpu.VMEM((width, out), bf16),
                dma((5,)),
            ]
            + [pltpu.VMEM((count, out), bf16)] * 6
            + [
                pltpu.VMEM((2, rows, WIDE), f32),
                pltpu.VMEM((2, rows // 2, WIDE), f32),
                pltpu.VMEM((2, rows // 2, WIDE), f32),
                pltpu.VMEM((2, ny - 1, quarter, WIDE), f32),
                pltpu.VMEM((2, quarter, WIDE), f32),
                pltpu.VMEM((2, eighth, WIDE), f32),
                pltpu.VMEM((2, eighth, WIDE), f32),
                pltpu.VMEM((2, eighth, WIDE), f32),
                pltpu.VMEM((2, eighth, WIDE), f32),
                pltpu.VMEM((2, rows, WIDE), f32),
            ]
            + sems,
            compiler_params=pltpu.CompilerParams(
                collective_id=0, has_side_effects=True, vmem_limit_bytes=60 * 1024 * 1024
            ),
        )(tokens, tangents, w_query, w_key, w_value))

    both = P(("tm", "space"), None)
    return jax.shard_map(
        step, mesh=mesh, in_specs=(both, both, P(), P(), P()), out_specs=(both, both),
        check_vma=False,
    )
```

```python
import functools

import jax
import jax.numpy as jnp
from jax import lax
from jax.experimental import pallas as pl
from jax.experimental.pallas import tpu as pltpu
from jax.sharding import PartitionSpec as P

HD = 112
HEADS = 5
WIDE = 128
EPSILON = 1e-06
MESH = pl.DeviceIdType.MESH


def dot(a, b, dims=((1,), (0,))):
    return lax.dot_general(a, b, (dims, ((), ())), preferred_element_type=jnp.float32)


def kernel(
    n_tm, n_space, rows,
    tok_hbm, tan_hbm, wq_hbm, wk_hbm, wv_hbm,
    att_ref, att_t_ref,
    tok, tan, wq, wk, wv, load_sem,
    kbuf, vbuf, ktbuf, vtbuf, qbuf, qtbuf,
    state, r1, abuf, r2, bbuf, r3, erecv, esend, xsend, full,
    s1, q1, s2, q2, s3, q3, s4, q4, s5, q5, s6, q6, s7, q7,
):
    ny, nz = n_space // 2, n_tm // 2
    half, quarter, eighth = rows // 2, rows // n_space, rows // (2 * n_space)
    tm, space = lax.axis_index("tm"), lax.axis_index("space")
    core, y = lax.rem(space, 2), space // 2
    x, z = lax.rem(tm, 2), tm // 2
    core_mate = space + 1 - 2 * core
    x_mate = tm + 1 - 2 * x
    z_next, z_prev = lax.rem(tm + 2, n_tm), lax.rem(tm + n_tm - 2, n_tm)

    def y_mate(k):
        return 2 * lax.rem(y + k, ny) + core

    def load(i, src, dst):
        return pltpu.make_async_copy(src, dst, load_sem.at[i])

    loads = [
        load(0, tok_hbm, tok), load(1, wk_hbm, wk), load(2, wv_hbm, wv),
        load(3, tan_hbm, tan), load(4, wq_hbm, wq),
    ]
    for one in loads:
        one.start()

    barrier = pltpu.get_barrier_semaphore()
    partners = [{"space": core_mate}, {"tm": x_mate}, {"tm": z_next}, {"tm": z_prev}]
    partners += [{"space": y_mate(k)} for k in range(1, ny)]
    for partner in partners:
        pl.semaphore_signal(barrier, inc=1, device_id=partner, device_id_type=MESH)

    def rows_at(start, count):
        return pl.ds(pl.multiple_of(start, 8), count)

    half_mine = core * half
    quarter_mine = half_mine + y * quarter

    def send(src, dst, ssem, rsem, device):
        return pltpu.make_async_remote_copy(
            src_ref=src, dst_ref=dst, send_sem=ssem, recv_sem=rsem,
            device_id=device, device_id_type=MESH,
        )

    def copy1(g):
        return send(
            state.at[g, rows_at((1 - core) * half, half)], r1.at[g],
            s1.at[g], q1.at[g], {"space": core_mate},
        )

    def copy2(g, k):
        return send(
            abuf.at[g, rows_at(lax.rem(y + k, ny) * quarter, quarter)], r2.at[g, k - 1],
            s2.at[g, k - 1], q2.at[g, k - 1], {"space": y_mate(k)},
        )

    def copy3(g):
        return send(
            bbuf.at[g, rows_at((1 - x) * eighth, eighth)], r3.at[g],
            s3.at[g], q3.at[g], {"tm": x_mate},
        )

    def copy4(g):
        return send(esend.at[g], erecv.at[g], s4.at[g], q4.at[g], {"tm": z_next})

    def copy5(g):
        return send(
            xsend.at[g], full.at[g, rows_at(quarter_mine + x * eighth, eighth)],
            s5.at[g], q5.at[g], {"tm": x_mate},
        )

    def copy6(g, k):
        part = full.at[g, rows_at(quarter_mine, quarter)]
        return send(part, part, s6.at[g, k - 1], q6.at[g, k - 1], {"space": y_mate(k)})

    def copy7(g, k):
        part = full.at[g, rows_at(half_mine + lax.rem(y + ny - k, ny) * quarter, quarter)]
        return send(part, part, s7.at[g, k], q7.at[g, k], {"space": core_mate})

    def stage1(g):
        copy1(g).start()

    def stage2(g):
        copy1(g).wait_recv()
        abuf[g] = state[g, rows_at(half_mine, half)] + r1[g]
        for k in range(1, ny):
            copy2(g, k).start()

    def stage3(g):
        total = abuf[g, rows_at(y * quarter, quarter)]
        for k in range(1, ny):
            copy2(g, k).wait_recv()
            total = total + r2[g, k - 1]
        bbuf[g] = total
        copy3(g).start()

    def stage4(g):
        copy3(g).wait_recv()
        own = bbuf[g, rows_at(x * eighth, eighth)]

        @pl.when(z == 0)
        def _():
            erecv[g] = jnp.zeros((eighth, WIDE), jnp.float32)

        @pl.when(z > 0)
        def _():
            copy4(g).wait_recv()

        before, other = erecv[g], r3[g]
        first = before + other
        pair = first + own

        @pl.when(z < nz - 1)
        def _():
            esend[g] = pair
            copy4(g).start()

        mine_first = x == 0
        xsend[g] = jnp.where(mine_first, pair, first)
        copy5(g).start()
        full[g, rows_at(quarter_mine + x * eighth, eighth)] = jnp.where(
            mine_first, before + own, pair
        )

    def stage6(g):
        copy5(g).wait_recv()
        for k in range(1, ny):
            copy6(g, k).start()
        copy7(g, 0).start()

    def stage7(g):
        for k in range(1, ny):
            copy6(g, k).wait_recv()
            copy7(g, k).start()

    def finish(g):
        for k in range(ny):
            copy7(g, k).wait_recv()

    def drain(g):
        copy1(g).wait_send()
        for k in range(1, ny):
            copy2(g, k).wait_send()
            copy6(g, k).wait_send()
        copy3(g).wait_send()

        @pl.when(z < nz - 1)
        def _():
            copy4(g).wait_send()

        copy5(g).wait_send()
        for k in range(ny):
            copy7(g, k).wait_send()

    def project(source, weight, out):
        out[...] = dot(weight[...], source[...]).astype(jnp.bfloat16)

    count = tok.shape[1]

    def head(ref, h):
        return ref[h * HD : (h + 1) * HD]

    first_row = lax.broadcasted_iota(jnp.int32, (WIDE - HD, count), 0) == 0

    def values_of(ref, h, fill):
        tail = jnp.where(first_row, fill, 0.0).astype(jnp.bfloat16)
        return jnp.concatenate([head(ref, h), tail], axis=0)

    for g in range(2):
        state[g, rows_at(HEADS * HD, rows - HEADS * HD)] = jnp.zeros(
            (rows - HEADS * HD, WIDE), jnp.float32
        )
    loads[0].wait()
    loads[1].wait()
    project(tok, wk, kbuf)
    loads[2].wait()
    project(tok, wv, vbuf)
    over = ((1,), (1,))
    zero = jnp.zeros((), jnp.bfloat16)
    for h in range(HEADS):
        feature = jnp.maximum(head(kbuf, h), zero)
        state[0, h * HD : (h + 1) * HD] = dot(feature, values_of(vbuf, h, 1.0), over)
    pl.semaphore_wait(barrier, len(partners))
    stage1(0)
    loads[3].wait()
    project(tan, wk, ktbuf)
    stage2(0)
    project(tan, wv, vtbuf)
    for h in range(HEADS):
        keys = head(kbuf, h)
        feature = jnp.maximum(keys, zero)
        slope = jnp.where(keys > 0, head(ktbuf, h), zero)
        state[1, h * HD : (h + 1) * HD] = dot(slope, values_of(vbuf, h, 1.0), over) + dot(
            feature, values_of(vtbuf, h, 0.0), over
        )
    stage1(1)
    stage3(0)
    loads[4].wait()
    project(tok, wq, qbuf)
    stage2(1)
    stage4(0)
    project(tan, wq, qtbuf)
    stage3(1)
    stage4(1)
    stage6(0)
    stage7(0)
    stage6(1)
    finish(0)
    stage7(1)
    finish(1)

    empty = jnp.zeros((HD, WIDE), jnp.float32)
    for h in range(HEADS):
        queries = head(qbuf, h)
        feature = jnp.maximum(queries, zero)
        slope = jnp.where(queries > 0, head(qtbuf, h), zero)
        sides = jnp.concatenate([feature, slope], axis=0)
        seen, seen_t = head(full.at[0], h), head(full.at[1], h)
        maps = jnp.concatenate(
            [
                jnp.concatenate([seen, seen_t], axis=1),
                jnp.concatenate([empty, seen], axis=1),
            ],
            axis=0,
        )
        high = maps.astype(jnp.bfloat16)
        low = (maps - high.astype(jnp.float32)).astype(jnp.bfloat16)
        across = ((0,), (0,))
        both = dot(high, sides, across) + dot(low, sides, across)
        main, slant = both[:WIDE], both[WIDE:]
        inverse = 1.0 / (main[HD : HD + 1] + EPSILON)
        denom_t = slant[HD : HD + 1]
        attended = main[:HD] * inverse
        tangent = (slant[:HD] - attended * denom_t) * inverse
        att_ref[h * HD : (h + 1) * HD] = attended.astype(att_ref.dtype)
        att_t_ref[h * HD : (h + 1) * HD] = tangent.astype(att_t_ref.dtype)
    for g in range(2):
        drain(g)


def solution(mesh):
    n_tm, n_space = mesh.shape["tm"], mesh.shape["space"]
    ny = n_space // 2
    unit = 8 * 2 * n_space
    rows = (HEADS * HD + unit) // unit * unit

    def step(tokens, tangents, w_query, w_key, w_value):
        count, width = tokens.shape
        out = w_query.shape[1]
        bf16, f32 = jnp.bfloat16, jnp.float32
        quarter, eighth = rows // n_space, rows // (2 * n_space)
        dma = pltpu.SemaphoreType.DMA
        sems = []
        for shape in ((2,), (2, ny - 1), (2,), (2,), (2,), (2, ny - 1), (2, ny)):
            sems += [dma(shape), dma(shape)]
        outs = pl.pallas_call(
            functools.partial(kernel, n_tm, n_space, rows),
            out_shape=[jax.ShapeDtypeStruct((out, count), bf16)] * 2,
            in_specs=[pl.BlockSpec(memory_space=pl.ANY)] * 5,
            out_specs=[pl.BlockSpec(memory_space=pltpu.VMEM)] * 2,
            scratch_shapes=[
                pltpu.VMEM((width, count), bf16),
                pltpu.VMEM((width, count), bf16),
                pltpu.VMEM((out, width), bf16),
                pltpu.VMEM((out, width), bf16),
                pltpu.VMEM((out, width), bf16),
                dma((5,)),
            ]
            + [pltpu.VMEM((out, count), bf16)] * 6
            + [
                pltpu.VMEM((2, rows, WIDE), f32),
                pltpu.VMEM((2, rows // 2, WIDE), f32),
                pltpu.VMEM((2, rows // 2, WIDE), f32),
                pltpu.VMEM((2, ny - 1, quarter, WIDE), f32),
                pltpu.VMEM((2, quarter, WIDE), f32),
                pltpu.VMEM((2, eighth, WIDE), f32),
                pltpu.VMEM((2, eighth, WIDE), f32),
                pltpu.VMEM((2, eighth, WIDE), f32),
                pltpu.VMEM((2, eighth, WIDE), f32),
                pltpu.VMEM((2, rows, WIDE), f32),
            ]
            + sems,
            compiler_params=pltpu.CompilerParams(
                collective_id=0, has_side_effects=True, vmem_limit_bytes=60 * 1024 * 1024
            ),
        )(tokens.T, tangents.T, w_query.T, w_key.T, w_value.T)
        return outs[0].T, outs[1].T

    both = P(("tm", "space"), None)
    return jax.shard_map(
        step, mesh=mesh, in_specs=(both, both, P(), P(), P()), out_specs=(both, both),
        check_vma=False,
    )
```

```python
import functools

import jax
import jax.numpy as jnp
from jax import lax
from jax.experimental import pallas as pl
from jax.experimental.pallas import tpu as pltpu
from jax.sharding import PartitionSpec as P

HD = 112
HEADS = 5
WIDE = 128
EPSILON = 1e-06
MESH = pl.DeviceIdType.MESH


def dot(a, b, dims=((1,), (0,))):
    return lax.dot_general(a, b, (dims, ((), ())), preferred_element_type=jnp.float32)


def kernel(
    n_tm, n_space, rows,
    tok_hbm, tan_hbm, wq_hbm, wk_hbm, wv_hbm,
    att_ref, att_t_ref,
    tok, tan, wq, wk, wv, load_sem,
    kbuf, vbuf, ktbuf, vtbuf, qbuf, qtbuf,
    state, r1, abuf, r2, bbuf, r3, erecv, esend, xsend, full, slant, ratios, inverses,
    s1, q1, s2, q2, s3, q3, s4, q4, s5, q5, s6, q6, s7, q7,
):
    ny, nz = n_space // 2, n_tm // 2
    half, quarter, eighth = rows // 2, rows // n_space, rows // (2 * n_space)
    tm, space = lax.axis_index("tm"), lax.axis_index("space")
    core, y = lax.rem(space, 2), space // 2
    x, z = lax.rem(tm, 2), tm // 2
    core_mate = space + 1 - 2 * core
    x_mate = tm + 1 - 2 * x
    z_next, z_prev = lax.rem(tm + 2, n_tm), lax.rem(tm + n_tm - 2, n_tm)

    def y_mate(k):
        return 2 * lax.rem(y + k, ny) + core

    def load(i, src, dst):
        return pltpu.make_async_copy(src, dst, load_sem.at[i])

    loads = [
        load(0, tok_hbm, tok), load(1, wk_hbm, wk), load(2, wv_hbm, wv),
        load(3, tan_hbm, tan), load(4, wq_hbm, wq),
    ]
    loads[0].start()
    loads[1].start()

    barrier = pltpu.get_barrier_semaphore()
    partners = [{"space": core_mate}, {"tm": x_mate}, {"tm": z_next}, {"tm": z_prev}]
    partners += [{"space": y_mate(k)} for k in range(1, ny)]
    for partner in partners:
        pl.semaphore_signal(barrier, inc=1, device_id=partner, device_id_type=MESH)

    def rows_at(start, count):
        return pl.ds(pl.multiple_of(start, 8), count)

    half_mine = core * half
    quarter_mine = half_mine + y * quarter

    def send(src, dst, ssem, rsem, device):
        return pltpu.make_async_remote_copy(
            src_ref=src, dst_ref=dst, send_sem=ssem, recv_sem=rsem,
            device_id=device, device_id_type=MESH,
        )

    def copy1(g):
        return send(
            state.at[g, rows_at((1 - core) * half, half)], r1.at[g],
            s1.at[g], q1.at[g], {"space": core_mate},
        )

    def copy2(g, k):
        return send(
            abuf.at[g, rows_at(lax.rem(y + k, ny) * quarter, quarter)], r2.at[g, k - 1],
            s2.at[g, k - 1], q2.at[g, k - 1], {"space": y_mate(k)},
        )

    def copy3(g):
        return send(
            bbuf.at[g, rows_at((1 - x) * eighth, eighth)], r3.at[g],
            s3.at[g], q3.at[g], {"tm": x_mate},
        )

    def copy4(g):
        return send(esend.at[g], erecv.at[g], s4.at[g], q4.at[g], {"tm": z_next})

    def copy5(g):
        return send(
            xsend.at[g], full.at[g, rows_at(quarter_mine + x * eighth, eighth)],
            s5.at[g], q5.at[g], {"tm": x_mate},
        )

    def copy6(g, k):
        part = full.at[g, rows_at(quarter_mine, quarter)]
        return send(part, part, s6.at[g, k - 1], q6.at[g, k - 1], {"space": y_mate(k)})

    def copy7(g, k):
        part = full.at[g, rows_at(half_mine + lax.rem(y + ny - k, ny) * quarter, quarter)]
        return send(part, part, s7.at[g, k], q7.at[g, k], {"space": core_mate})

    def stage1(g):
        copy1(g).start()

    def stage2(g):
        copy1(g).wait_recv()
        abuf[g] = state[g, rows_at(half_mine, half)] + r1[g]
        for k in range(1, ny):
            copy2(g, k).start()

    def stage3(g):
        total = abuf[g, rows_at(y * quarter, quarter)]
        for k in range(1, ny):
            copy2(g, k).wait_recv()
            total = total + r2[g, k - 1]
        bbuf[g] = total
        copy3(g).start()

    def stage4(g):
        copy3(g).wait_recv()
        own = bbuf[g, rows_at(x * eighth, eighth)]

        @pl.when(z == 0)
        def _():
            erecv[g] = jnp.zeros((eighth, WIDE), jnp.float32)

        @pl.when(z > 0)
        def _():
            copy4(g).wait_recv()

        before, other = erecv[g], r3[g]
        first = before + other
        pair = first + own

        @pl.when(z < nz - 1)
        def _():
            esend[g] = pair
            copy4(g).start()

        mine_first = x == 0
        xsend[g] = jnp.where(mine_first, pair, first)
        copy5(g).start()
        full[g, rows_at(quarter_mine + x * eighth, eighth)] = jnp.where(
            mine_first, before + own, pair
        )

    def stage6(g):
        copy5(g).wait_recv()
        for k in range(1, ny):
            copy6(g, k).start()
        copy7(g, 0).start()

    def stage7(g):
        for k in range(1, ny):
            copy6(g, k).wait_recv()
            copy7(g, k).start()

    def finish(g):
        for k in range(ny):
            copy7(g, k).wait_recv()

    def drain(g):
        copy1(g).wait_send()
        for k in range(1, ny):
            copy2(g, k).wait_send()
            copy6(g, k).wait_send()
        copy3(g).wait_send()

        @pl.when(z < nz - 1)
        def _():
            copy4(g).wait_send()

        copy5(g).wait_send()
        for k in range(ny):
            copy7(g, k).wait_send()

    def project(source, weight, out):
        out[...] = dot(weight[...], source[...]).astype(jnp.bfloat16)

    count = tok.shape[1]

    def head(ref, h):
        return ref[h * HD : (h + 1) * HD]

    first_row = lax.broadcasted_iota(jnp.int32, (WIDE - HD, count), 0) == 0

    def values_of(ref, h, fill):
        tail = jnp.where(first_row, fill, 0.0).astype(jnp.bfloat16)
        return jnp.concatenate([head(ref, h), tail], axis=0)

    for g in range(2):
        state[g, rows_at(HEADS * HD, rows - HEADS * HD)] = jnp.zeros(
            (rows - HEADS * HD, WIDE), jnp.float32
        )
    loads[0].wait()
    loads[1].wait()
    loads[2].start()
    loads[3].start()
    project(tok, wk, kbuf)
    loads[2].wait()
    loads[4].start()
    project(tok, wv, vbuf)
    over = ((1,), (1,))
    zero = jnp.zeros((), jnp.bfloat16)
    for h in range(HEADS):
        feature = jnp.maximum(head(kbuf, h), zero)
        state[0, h * HD : (h + 1) * HD] = dot(feature, values_of(vbuf, h, 1.0), over)
    pl.semaphore_wait(barrier, len(partners))
    stage1(0)
    loads[3].wait()
    project(tan, wk, ktbuf)
    stage2(0)
    project(tan, wv, vtbuf)
    for h in range(HEADS):
        keys = head(kbuf, h)
        feature = jnp.maximum(keys, zero)
        slope = jnp.where(keys > 0, head(ktbuf, h), zero)
        state[1, h * HD : (h + 1) * HD] = dot(slope, values_of(vbuf, h, 1.0), over) + dot(
            feature, values_of(vtbuf, h, 0.0), over
        )
    stage1(1)
    stage3(0)
    loads[4].wait()
    project(tok, wq, qbuf)
    stage2(1)
    stage4(0)
    project(tan, wq, qtbuf)
    stage3(1)
    stage4(1)
    stage6(0)
    stage7(0)
    stage6(1)
    finish(0)

    across = ((0,), (0,))

    def maps_of(g, h):
        seen = head(full.at[g], h)
        high = seen.astype(jnp.bfloat16)
        low = (seen - high.astype(jnp.float32)).astype(jnp.bfloat16)
        return jnp.concatenate([high, low], axis=0)

    def twice(a):
        return jnp.concatenate([a, a], axis=0)

    for h in range(HEADS):
        queries = head(qbuf, h)
        slope = jnp.where(queries > 0, head(qtbuf, h), zero)
        maps = maps_of(0, h)
        main = dot(maps, twice(jnp.maximum(queries, zero)), across)
        slant[h] = dot(maps, twice(slope), across)
        inverse = 1.0 / (main[HD : HD + 1] + EPSILON)
        ratio = main[:HD] * inverse
        inverses[h] = jnp.broadcast_to(inverse, inverses.shape[1:])
        ratios[h] = ratio
        att_ref[h * HD : (h + 1) * HD] = ratio.astype(att_ref.dtype)
    stage7(1)
    finish(1)
    for h in range(HEADS):
        feature = jnp.maximum(head(qbuf, h), zero)
        change = slant[h] + dot(maps_of(1, h), twice(feature), across)
        tangent = (change[:HD] - ratios[h] * change[HD : HD + 1]) * inverses[h, :1]
        att_t_ref[h * HD : (h + 1) * HD] = tangent.astype(att_t_ref.dtype)
    for g in range(2):
        drain(g)


def solution(mesh):
    n_tm, n_space = mesh.shape["tm"], mesh.shape["space"]
    ny = n_space // 2
    unit = 8 * 2 * n_space
    rows = (HEADS * HD + unit) // unit * unit

    def step(tokens, tangents, w_query, w_key, w_value):
        count, width = tokens.shape
        out = w_query.shape[1]
        bf16, f32 = jnp.bfloat16, jnp.float32
        quarter, eighth = rows // n_space, rows // (2 * n_space)
        dma = pltpu.SemaphoreType.DMA
        sems = []
        for shape in ((2,), (2, ny - 1), (2,), (2,), (2,), (2, ny - 1), (2, ny)):
            sems += [dma(shape), dma(shape)]
        outs = pl.pallas_call(
            functools.partial(kernel, n_tm, n_space, rows),
            out_shape=[pltpu.VMEM((out, count), bf16)] * 2,
            in_specs=[pl.BlockSpec(memory_space=pltpu.HBM)] * 5,
            out_specs=[pl.BlockSpec(memory_space=pltpu.VMEM)] * 2,
            scratch_shapes=[
                pltpu.VMEM((width, count), bf16),
                pltpu.VMEM((width, count), bf16),
                pltpu.VMEM((out, width), bf16),
                pltpu.VMEM((out, width), bf16),
                pltpu.VMEM((out, width), bf16),
                dma((5,)),
            ]
            + [pltpu.VMEM((out, count), bf16)] * 6
            + [
                pltpu.VMEM((2, rows, WIDE), f32),
                pltpu.VMEM((2, rows // 2, WIDE), f32),
                pltpu.VMEM((2, rows // 2, WIDE), f32),
                pltpu.VMEM((2, ny - 1, quarter, WIDE), f32),
                pltpu.VMEM((2, quarter, WIDE), f32),
                pltpu.VMEM((2, eighth, WIDE), f32),
                pltpu.VMEM((2, eighth, WIDE), f32),
                pltpu.VMEM((2, eighth, WIDE), f32),
                pltpu.VMEM((2, eighth, WIDE), f32),
                pltpu.VMEM((2, rows, WIDE), f32),
                pltpu.VMEM((HEADS, WIDE, count), f32),
                pltpu.VMEM((HEADS, HD, count), f32),
                pltpu.VMEM((HEADS, 8, count), f32),
            ]
            + sems,
            compiler_params=pltpu.CompilerParams(
                collective_id=0, has_side_effects=True, vmem_limit_bytes=57 * 1024 * 1024
            ),
        )(tokens.T, tangents.T, w_query.T, w_key.T, w_value.T)
        return outs[0].T, outs[1].T

    both = P(("tm", "space"), None)
    return jax.shard_map(
        step, mesh=mesh, in_specs=(both, both, P(), P(), P()), out_specs=(both, both),
        check_vma=False,
    )
```

```python
import functools

import jax
import jax.numpy as jnp
from jax import lax
from jax.experimental import pallas as pl
from jax.experimental.pallas import tpu as pltpu
from jax.sharding import PartitionSpec as P

HD = 112
HEADS = 5
WIDE = 128
EPSILON = 1e-06
MESH = pl.DeviceIdType.MESH


def dot(a, b, dims=((1,), (0,))):
    return lax.dot_general(a, b, (dims, ((), ())), preferred_element_type=jnp.float32)


def kernel(
    n_tm, n_space, rows,
    tok_hbm, tan_hbm, wq_hbm, wk_hbm, wv_hbm,
    att_ref, att_t_ref,
    tok, tan, wq, wk, wv, load_sem,
    kbuf, vbuf, ktbuf, vtbuf, qbuf, qtbuf,
    state, r1, abuf, r2, bbuf, r3, erecv, esend, xsend, full, slant, ratios, inverses,
    s1, q1, s2, q2, s3, q3, s4, q4, s5, q5, s6, q6, s7, q7,
):
    ny, nz = n_space // 2, n_tm // 2
    half, quarter, eighth = rows // 2, rows // n_space, rows // (2 * n_space)
    tm, space = lax.axis_index("tm"), lax.axis_index("space")
    core, y = lax.rem(space, 2), space // 2
    x, z = lax.rem(tm, 2), tm // 2
    core_mate = space + 1 - 2 * core
    x_mate = tm + 1 - 2 * x
    z_next, z_prev = lax.rem(tm + 2, n_tm), lax.rem(tm + n_tm - 2, n_tm)

    def y_mate(k):
        return 2 * lax.rem(y + k, ny) + core

    def load(i, src, dst):
        return pltpu.make_async_copy(src, dst, load_sem.at[i])

    loads = [
        load(0, tok_hbm, tok), load(1, wk_hbm, wk), load(2, wv_hbm, wv),
        load(3, tan_hbm, tan), load(4, wq_hbm, wq),
    ]
    loads[0].start()
    loads[1].start()

    barrier = pltpu.get_barrier_semaphore()
    partners = [{"space": core_mate}, {"tm": x_mate}, {"tm": z_next}, {"tm": z_prev}]
    partners += [{"space": y_mate(k)} for k in range(1, ny)]
    for partner in partners:
        pl.semaphore_signal(barrier, inc=1, device_id=partner, device_id_type=MESH)

    def rows_at(start, count):
        return pl.ds(pl.multiple_of(start, 8), count)

    half_mine = core * half
    quarter_mine = half_mine + y * quarter

    def send(src, dst, ssem, rsem, device):
        return pltpu.make_async_remote_copy(
            src_ref=src, dst_ref=dst, send_sem=ssem, recv_sem=rsem,
            device_id=device, device_id_type=MESH,
        )

    def copy1(g):
        return send(
            state.at[g, rows_at((1 - core) * half, half)], r1.at[g],
            s1.at[g], q1.at[g], {"space": core_mate},
        )

    def copy2(g, k):
        return send(
            abuf.at[g, rows_at(lax.rem(y + k, ny) * quarter, quarter)], r2.at[g, k - 1],
            s2.at[g, k - 1], q2.at[g, k - 1], {"space": y_mate(k)},
        )

    def copy3(g):
        return send(
            bbuf.at[g, rows_at((1 - x) * eighth, eighth)], r3.at[g],
            s3.at[g], q3.at[g], {"tm": x_mate},
        )

    cut = (eighth // 8 + 1) // 2 * 8
    pieces = [(0, cut), (cut, eighth - cut)]

    def copy4(g, j):
        part = pl.ds(*pieces[j])
        return send(
            esend.at[g, part], erecv.at[g, part], s4.at[g, j], q4.at[g, j], {"tm": z_next}
        )

    def copy5(g, j):
        start, size = pieces[j]
        return send(
            xsend.at[g, pl.ds(start, size)],
            full.at[g, rows_at(quarter_mine + x * eighth + start, size)],
            s5.at[g, j], q5.at[g, j], {"tm": x_mate},
        )

    def copy6(g, k):
        part = full.at[g, rows_at(quarter_mine, quarter)]
        return send(part, part, s6.at[g, k - 1], q6.at[g, k - 1], {"space": y_mate(k)})

    def copy7(g, k):
        part = full.at[g, rows_at(half_mine + lax.rem(y + ny - k, ny) * quarter, quarter)]
        return send(part, part, s7.at[g, k], q7.at[g, k], {"space": core_mate})

    def stage1(g):
        copy1(g).start()

    def stage2(g):
        copy1(g).wait_recv()
        abuf[g] = state[g, rows_at(half_mine, half)] + r1[g]
        for k in range(1, ny):
            copy2(g, k).start()

    def stage3(g):
        total = abuf[g, rows_at(y * quarter, quarter)]
        for k in range(1, ny):
            copy2(g, k).wait_recv()
            total = total + r2[g, k - 1]
        bbuf[g] = total
        copy3(g).start()

    def stage4(g):
        copy3(g).wait_recv()
        for j, (start, size) in enumerate(pieces):
            piece(g, j, start, size)

    def piece(g, j, start, size):
        part = pl.ds(start, size)
        own = bbuf[g, rows_at(x * eighth + start, size)]

        @pl.when(z == 0)
        def _():
            erecv[g, part] = jnp.zeros((size, WIDE), jnp.float32)

        @pl.when(z > 0)
        def _():
            copy4(g, j).wait_recv()

        before, other = erecv[g, part], r3[g, part]
        first = before + other
        pair = first + own

        @pl.when(z < nz - 1)
        def _():
            esend[g, part] = pair
            copy4(g, j).start()

        mine_first = x == 0
        xsend[g, part] = jnp.where(mine_first, pair, first)
        copy5(g, j).start()
        full[g, rows_at(quarter_mine + x * eighth + start, size)] = jnp.where(
            mine_first, before + own, pair
        )

    def stage6(g):
        for j in range(2):
            copy5(g, j).wait_recv()
        for k in range(1, ny):
            copy6(g, k).start()
        copy7(g, 0).start()

    def stage7(g):
        for k in range(1, ny):
            copy6(g, k).wait_recv()
            copy7(g, k).start()

    def finish(g):
        for k in range(ny):
            copy7(g, k).wait_recv()

    def drain(g):
        copy1(g).wait_send()
        for k in range(1, ny):
            copy2(g, k).wait_send()
            copy6(g, k).wait_send()
        copy3(g).wait_send()

        @pl.when(z < nz - 1)
        def _():
            for j in range(2):
                copy4(g, j).wait_send()

        for j in range(2):
            copy5(g, j).wait_send()
        for k in range(ny):
            copy7(g, k).wait_send()

    def project(source, weight, out):
        out[...] = dot(weight[...], source[...]).astype(jnp.bfloat16)

    count = tok.shape[1]

    def head(ref, h):
        return ref[h * HD : (h + 1) * HD]

    first_row = lax.broadcasted_iota(jnp.int32, (WIDE - HD, count), 0) == 0

    def values_of(ref, h, fill):
        tail = jnp.where(first_row, fill, 0.0).astype(jnp.bfloat16)
        return jnp.concatenate([head(ref, h), tail], axis=0)

    for g in range(2):
        state[g, rows_at(HEADS * HD, rows - HEADS * HD)] = jnp.zeros(
            (rows - HEADS * HD, WIDE), jnp.float32
        )
    loads[0].wait()
    loads[1].wait()
    loads[2].start()
    loads[3].start()
    project(tok, wk, kbuf)
    loads[2].wait()
    loads[4].start()
    project(tok, wv, vbuf)
    over = ((1,), (1,))
    zero = jnp.zeros((), jnp.bfloat16)
    for h in range(HEADS):
        feature = jnp.maximum(head(kbuf, h), zero)
        state[0, h * HD : (h + 1) * HD] = dot(feature, values_of(vbuf, h, 1.0), over)
    pl.semaphore_wait(barrier, len(partners))
    stage1(0)
    loads[3].wait()
    project(tan, wk, ktbuf)
    stage2(0)
    project(tan, wv, vtbuf)
    for h in range(HEADS):
        keys = head(kbuf, h)
        feature = jnp.maximum(keys, zero)
        slope = jnp.where(keys > 0, head(ktbuf, h), zero)
        state[1, h * HD : (h + 1) * HD] = dot(slope, values_of(vbuf, h, 1.0), over) + dot(
            feature, values_of(vtbuf, h, 0.0), over
        )
    stage1(1)
    stage3(0)
    loads[4].wait()
    project(tok, wq, qbuf)
    stage2(1)
    stage4(0)
    project(tan, wq, qtbuf)
    stage3(1)
    stage4(1)
    stage6(0)
    stage7(0)
    stage6(1)
    finish(0)

    across = ((0,), (0,))

    def maps_of(g, h):
        seen = head(full.at[g], h)
        high = seen.astype(jnp.bfloat16)
        low = (seen - high.astype(jnp.float32)).astype(jnp.bfloat16)
        return jnp.concatenate([high, low], axis=0)

    def twice(a):
        return jnp.concatenate([a, a], axis=0)

    for h in range(HEADS):
        queries = head(qbuf, h)
        slope = jnp.where(queries > 0, head(qtbuf, h), zero)
        maps = maps_of(0, h)
        main = dot(maps, twice(jnp.maximum(queries, zero)), across)
        slant[h] = dot(maps, twice(slope), across)
        inverse = 1.0 / (main[HD : HD + 1] + EPSILON)
        ratio = main[:HD] * inverse
        inverses[h] = jnp.broadcast_to(inverse, inverses.shape[1:])
        ratios[h] = ratio
        att_ref[h * HD : (h + 1) * HD] = ratio.astype(att_ref.dtype)
    stage7(1)
    finish(1)
    for h in range(HEADS):
        feature = jnp.maximum(head(qbuf, h), zero)
        change = slant[h] + dot(maps_of(1, h), twice(feature), across)
        tangent = (change[:HD] - ratios[h] * change[HD : HD + 1]) * inverses[h, :1]
        att_t_ref[h * HD : (h + 1) * HD] = tangent.astype(att_t_ref.dtype)
    for g in range(2):
        drain(g)


def solution(mesh):
    n_tm, n_space = mesh.shape["tm"], mesh.shape["space"]
    ny = n_space // 2
    unit = 8 * 2 * n_space
    rows = (HEADS * HD + unit) // unit * unit

    def step(tokens, tangents, w_query, w_key, w_value):
        count, width = tokens.shape
        out = w_query.shape[1]
        bf16, f32 = jnp.bfloat16, jnp.float32
        quarter, eighth = rows // n_space, rows // (2 * n_space)
        dma = pltpu.SemaphoreType.DMA
        sems = []
        for shape in ((2,), (2, ny - 1), (2,), (2, 2), (2, 2), (2, ny - 1), (2, ny)):
            sems += [dma(shape), dma(shape)]
        outs = pl.pallas_call(
            functools.partial(kernel, n_tm, n_space, rows),
            out_shape=[pltpu.VMEM((out, count), bf16)] * 2,
            in_specs=[pl.BlockSpec(memory_space=pltpu.HBM)] * 5,
            out_specs=[pl.BlockSpec(memory_space=pltpu.VMEM)] * 2,
            scratch_shapes=[
                pltpu.VMEM((width, count), bf16),
                pltpu.VMEM((width, count), bf16),
                pltpu.VMEM((out, width), bf16),
                pltpu.VMEM((out, width), bf16),
                pltpu.VMEM((out, width), bf16),
                dma((5,)),
            ]
            + [pltpu.VMEM((out, count), bf16)] * 6
            + [
                pltpu.VMEM((2, rows, WIDE), f32),
                pltpu.VMEM((2, rows // 2, WIDE), f32),
                pltpu.VMEM((2, rows // 2, WIDE), f32),
                pltpu.VMEM((2, ny - 1, quarter, WIDE), f32),
                pltpu.VMEM((2, quarter, WIDE), f32),
                pltpu.VMEM((2, eighth, WIDE), f32),
                pltpu.VMEM((2, eighth, WIDE), f32),
                pltpu.VMEM((2, eighth, WIDE), f32),
                pltpu.VMEM((2, eighth, WIDE), f32),
                pltpu.VMEM((2, rows, WIDE), f32),
                pltpu.VMEM((HEADS, WIDE, count), f32),
                pltpu.VMEM((HEADS, HD, count), f32),
                pltpu.VMEM((HEADS, 8, count), f32),
            ]
            + sems,
            compiler_params=pltpu.CompilerParams(
                collective_id=0, has_side_effects=True, vmem_limit_bytes=57 * 1024 * 1024
            ),
        )(tokens.T, tangents.T, w_query.T, w_key.T, w_value.T)
        return outs[0].T, outs[1].T

    both = P(("tm", "space"), None)
    return jax.shard_map(
        step, mesh=mesh, in_specs=(both, both, P(), P(), P()), out_specs=(both, both),
        check_vma=False,
    )
```

```python
import functools

import jax
import jax.numpy as jnp
from jax import lax
from jax.experimental import pallas as pl
from jax.experimental.pallas import tpu as pltpu
from jax.sharding import PartitionSpec as P

HD = 112
HEADS = 5
WIDE = 128
EPSILON = 1e-06
MESH = pl.DeviceIdType.MESH


def dot(a, b, dims=((1,), (0,))):
    return lax.dot_general(a, b, (dims, ((), ())), preferred_element_type=jnp.float32)


def kernel(
    n_tm, n_space, rows,
    tok_hbm, tan_hbm, wq_hbm, wk_hbm, wv_hbm,
    att_ref, att_t_ref,
    tok, tan, wq, wk, wv, load_sem,
    kbuf, vbuf, ktbuf, vtbuf, qbuf, qtbuf,
    state, r1, abuf, r2, bbuf, r3, erecv, esend, xsend, full, slant, ratios, inverses,
    s1, q1, s2, q2, s3, q3, s4, q4, s5, q5, s6, q6, s7, q7,
):
    ny, nz = n_space // 2, n_tm // 2
    half, quarter, eighth = rows // 2, rows // n_space, rows // (2 * n_space)
    tm, space = lax.axis_index("tm"), lax.axis_index("space")
    core, y = lax.rem(space, 2), space // 2
    x, z = lax.rem(tm, 2), tm // 2
    core_mate = space + 1 - 2 * core
    x_mate = tm + 1 - 2 * x
    z_next, z_prev = lax.rem(tm + 2, n_tm), lax.rem(tm + n_tm - 2, n_tm)

    def y_mate(k):
        return 2 * lax.rem(y + k, ny) + core

    def load(i, src, dst):
        return pltpu.make_async_copy(src, dst, load_sem.at[i])

    loads = [
        load(0, tok_hbm, tok), load(1, wk_hbm, wk), load(2, wv_hbm, wv),
        load(3, tan_hbm, tan), load(4, wq_hbm, wq),
    ]
    loads[0].start()
    loads[1].start()

    barrier = pltpu.get_barrier_semaphore()
    partners = [{"space": core_mate}, {"tm": x_mate}, {"tm": z_next}, {"tm": z_prev}]
    partners += [{"space": y_mate(k)} for k in range(1, ny)]
    for partner in partners:
        pl.semaphore_signal(barrier, inc=1, device_id=partner, device_id_type=MESH)

    def rows_at(start, count):
        return pl.ds(pl.multiple_of(start, 8), count)

    half_mine = core * half
    quarter_mine = half_mine + y * quarter

    def send(src, dst, ssem, rsem, device):
        return pltpu.make_async_remote_copy(
            src_ref=src, dst_ref=dst, send_sem=ssem, recv_sem=rsem,
            device_id=device, device_id_type=MESH,
        )

    def copy1(g):
        return send(
            state.at[g, rows_at((1 - core) * half, half)], r1.at[g],
            s1.at[g], q1.at[g], {"space": core_mate},
        )

    def copy2(g, k):
        return send(
            abuf.at[g, rows_at(lax.rem(y + k, ny) * quarter, quarter)], r2.at[g, k - 1],
            s2.at[g, k - 1], q2.at[g, k - 1], {"space": y_mate(k)},
        )

    def copy3(g):
        return send(
            bbuf.at[g, rows_at((1 - x) * eighth, eighth)], r3.at[g],
            s3.at[g], q3.at[g], {"tm": x_mate},
        )

    cut = (eighth // 8 + 1) // 2 * 8
    pieces = [(0, cut), (cut, eighth - cut)]

    def copy4(g, j):
        part = pl.ds(*pieces[j])
        return send(
            esend.at[g, part], erecv.at[g, part], s4.at[g, j], q4.at[g, j], {"tm": z_next}
        )

    def copy5(g, j):
        start, size = pieces[j]
        return send(
            xsend.at[g, pl.ds(start, size)],
            full.at[g, rows_at(quarter_mine + x * eighth + start, size)],
            s5.at[g, j], q5.at[g, j], {"tm": x_mate},
        )

    def copy6(g, k):
        part = full.at[g, rows_at(quarter_mine, quarter)]
        return send(part, part, s6.at[g, k - 1], q6.at[g, k - 1], {"space": y_mate(k)})

    def copy7(g, k):
        part = full.at[g, rows_at(half_mine + lax.rem(y + ny - k, ny) * quarter, quarter)]
        return send(part, part, s7.at[g, k], q7.at[g, k], {"space": core_mate})

    def stage1(g):
        copy1(g).start()

    def stage2(g):
        copy1(g).wait_recv()
        abuf[g] = state[g, rows_at(half_mine, half)] + r1[g]
        for k in range(1, ny):
            copy2(g, k).start()

    def stage3(g):
        total = abuf[g, rows_at(y * quarter, quarter)]
        for k in range(1, ny):
            copy2(g, k).wait_recv()
            total = total + r2[g, k - 1]
        bbuf[g] = total
        copy3(g).start()

    def stage4(g):
        copy3(g).wait_recv()
        for j, (start, size) in enumerate(pieces):
            piece(g, j, start, size)

    def piece(g, j, start, size):
        part = pl.ds(start, size)
        own = bbuf[g, rows_at(x * eighth + start, size)]

        @pl.when(z == 0)
        def _():
            erecv[g, part] = jnp.zeros((size, WIDE), jnp.float32)

        @pl.when(z > 0)
        def _():
            copy4(g, j).wait_recv()

        before, other = erecv[g, part], r3[g, part]
        first = before + other
        pair = first + own

        @pl.when(z < nz - 1)
        def _():
            esend[g, part] = pair
            copy4(g, j).start()

        mine_first = x == 0
        xsend[g, part] = jnp.where(mine_first, pair, first)
        copy5(g, j).start()
        full[g, rows_at(quarter_mine + x * eighth + start, size)] = jnp.where(
            mine_first, before + own, pair
        )

    def stage6(g):
        for j in range(2):
            copy5(g, j).wait_recv()
        for k in range(1, ny):
            copy6(g, k).start()
        copy7(g, 0).start()

    def stage7(g):
        for k in range(1, ny):
            copy6(g, k).wait_recv()
            copy7(g, k).start()

    def finish(g):
        for k in range(ny):
            copy7(g, k).wait_recv()

    def drain(g):
        copy1(g).wait_send()
        for k in range(1, ny):
            copy2(g, k).wait_send()
            copy6(g, k).wait_send()
        copy3(g).wait_send()

        @pl.when(z < nz - 1)
        def _():
            for j in range(2):
                copy4(g, j).wait_send()

        for j in range(2):
            copy5(g, j).wait_send()
        for k in range(ny):
            copy7(g, k).wait_send()

    def project(source, weight, out):
        out[...] = dot(weight[...], source[...]).astype(jnp.bfloat16)

    count = tok.shape[1]

    def head(ref, h):
        return ref[h * HD : (h + 1) * HD]

    first_row = lax.broadcasted_iota(jnp.int32, (WIDE - HD, count), 0) == 0

    def values_of(ref, h, fill):
        tail = jnp.where(first_row, fill, 0.0).astype(jnp.bfloat16)
        return jnp.concatenate([head(ref, h), tail], axis=0)

    for g in range(2):
        state[g, rows_at(HEADS * HD, rows - HEADS * HD)] = jnp.zeros(
            (rows - HEADS * HD, WIDE), jnp.float32
        )
    loads[0].wait()
    loads[1].wait()
    loads[2].start()
    loads[3].start()
    project(tok, wk, kbuf)
    loads[2].wait()
    loads[4].start()
    project(tok, wv, vbuf)
    over = ((1,), (1,))
    zero = jnp.zeros((), jnp.bfloat16)
    for h in range(HEADS):
        feature = jnp.maximum(head(kbuf, h), zero)
        state[0, h * HD : (h + 1) * HD] = dot(feature, values_of(vbuf, h, 1.0), over)
    pl.semaphore_wait(barrier, len(partners))
    stage1(0)
    loads[3].wait()
    project(tan, wk, ktbuf)
    stage2(0)
    project(tan, wv, vtbuf)
    for h in range(HEADS):
        keys = head(kbuf, h)
        feature = jnp.maximum(keys, zero)
        slope = jnp.where(keys > 0, head(ktbuf, h), zero)
        state[1, h * HD : (h + 1) * HD] = dot(slope, values_of(vbuf, h, 1.0), over) + dot(
            feature, values_of(vtbuf, h, 0.0), over
        )
    stage1(1)
    stage3(0)
    loads[4].wait()
    project(tok, wq, qbuf)
    stage2(1)
    project(tan, wq, qtbuf)
    stage3(1)
    stage4(0)
    stage4(1)
    stage6(0)
    stage7(0)
    stage6(1)
    finish(0)

    across = ((0,), (0,))

    def maps_of(g, h):
        seen = head(full.at[g], h)
        high = seen.astype(jnp.bfloat16)
        low = (seen - high.astype(jnp.float32)).astype(jnp.bfloat16)
        return jnp.concatenate([high, low], axis=0)

    def twice(a):
        return jnp.concatenate([a, a], axis=0)

    for h in range(HEADS):
        queries = head(qbuf, h)
        slope = jnp.where(queries > 0, head(qtbuf, h), zero)
        maps = maps_of(0, h)
        main = dot(maps, twice(jnp.maximum(queries, zero)), across)
        slant[h] = dot(maps, twice(slope), across)
        inverse = 1.0 / (main[HD : HD + 1] + EPSILON)
        ratio = main[:HD] * inverse
        inverses[h] = jnp.broadcast_to(inverse, inverses.shape[1:])
        ratios[h] = ratio
        att_ref[h * HD : (h + 1) * HD] = ratio.astype(att_ref.dtype)
    stage7(1)
    finish(1)
    for h in range(HEADS):
        feature = jnp.maximum(head(qbuf, h), zero)
        change = slant[h] + dot(maps_of(1, h), twice(feature), across)
        tangent = (change[:HD] - ratios[h] * change[HD : HD + 1]) * inverses[h, :1]
        att_t_ref[h * HD : (h + 1) * HD] = tangent.astype(att_t_ref.dtype)
    for g in range(2):
        drain(g)


def solution(mesh):
    n_tm, n_space = mesh.shape["tm"], mesh.shape["space"]
    ny = n_space // 2
    unit = 8 * 2 * n_space
    rows = (HEADS * HD + unit) // unit * unit

    def step(tokens, tangents, w_query, w_key, w_value):
        count, width = tokens.shape
        out = w_query.shape[1]
        bf16, f32 = jnp.bfloat16, jnp.float32
        quarter, eighth = rows // n_space, rows // (2 * n_space)
        dma = pltpu.SemaphoreType.DMA
        sems = []
        for shape in ((2,), (2, ny - 1), (2,), (2, 2), (2, 2), (2, ny - 1), (2, ny)):
            sems += [dma(shape), dma(shape)]
        outs = pl.pallas_call(
            functools.partial(kernel, n_tm, n_space, rows),
            out_shape=[pltpu.VMEM((out, count), bf16)] * 2,
            in_specs=[pl.BlockSpec(memory_space=pltpu.HBM)] * 5,
            out_specs=[pl.BlockSpec(memory_space=pltpu.VMEM)] * 2,
            scratch_shapes=[
                pltpu.VMEM((width, count), bf16),
                pltpu.VMEM((width, count), bf16),
                pltpu.VMEM((out, width), bf16),
                pltpu.VMEM((out, width), bf16),
                pltpu.VMEM((out, width), bf16),
                dma((5,)),
            ]
            + [pltpu.VMEM((out, count), bf16)] * 6
            + [
                pltpu.VMEM((2, rows, WIDE), f32),
                pltpu.VMEM((2, rows // 2, WIDE), f32),
                pltpu.VMEM((2, rows // 2, WIDE), f32),
                pltpu.VMEM((2, ny - 1, quarter, WIDE), f32),
                pltpu.VMEM((2, quarter, WIDE), f32),
                pltpu.VMEM((2, eighth, WIDE), f32),
                pltpu.VMEM((2, eighth, WIDE), f32),
                pltpu.VMEM((2, eighth, WIDE), f32),
                pltpu.VMEM((2, eighth, WIDE), f32),
                pltpu.VMEM((2, rows, WIDE), f32),
                pltpu.VMEM((HEADS, WIDE, count), f32),
                pltpu.VMEM((HEADS, HD, count), f32),
                pltpu.VMEM((HEADS, 8, count), f32),
            ]
            + sems,
            compiler_params=pltpu.CompilerParams(
                collective_id=0, has_side_effects=True, vmem_limit_bytes=57 * 1024 * 1024
            ),
        )(tokens.T, tangents.T, w_query.T, w_key.T, w_value.T)
        return outs[0].T, outs[1].T

    both = P(("tm", "space"), None)
    return jax.shard_map(
        step, mesh=mesh, in_specs=(both, both, P(), P(), P()), out_specs=(both, both),
        check_vma=False,
    )
```
